32 devices in a mesh: dp: 16 (over z, y, x), grp: 2 (over core).
Axes of the slice: x: 2, y: 2, z: 4, core: 2. Of those that a mesh axis runs over, the one named last changes fastest.
Arguments:
- query_features: bfloat16 [32768, 512], P(('dp', 'grp')), may hold values from -256 to 256
- query_weights: bfloat16 [32768], P(('dp', 'grp')), may hold values from 0.5 to 13.5, as said below
- positive_index: int32 [32768], P(('dp', 'grp')), may hold values from 0 to 511
- item_features: bfloat16 [512, 512], P(('dp', 'grp')), may hold values from -6 to 6
- item_ids: int32 [512], P(('dp', 'grp')), may hold values from 0 to 255
- item_logq: bfloat16 [512], P(('dp', 'grp')), may hold values from -14 to -11
- query_w_in: bfloat16 [512, 1024], replicated, may hold values from -0.25 to 0.25
- query_w_out: bfloat16 [1024, 256], replicated, may hold values from -0.1875 to 0.1875
- item_w_in: bfloat16 [512, 1024], replicated, may hold values from -0.25 to 0.25
- item_w_out: bfloat16 [1024, 256], replicated, may hold values from -0.1875 to 0.1875
Outputs:
- grad_query_w_in: float32 [512, 1024], replicated
- grad_query_w_out: float32 [1024, 256], replicated
- grad_item_w_in: float32 [512, 1024], replicated
- grad_item_w_out: float32 [1024, 256], replicated
The draws below stay inside these ranges and needn't reach their ends.
Inputs may be any that keep to these rules, and one draw needn't show every extreme that they name: `query_weights`: positive weights. `item_ids`: an id may occur several times in the sample set.
All inputs are finite; a program needn't handle non-finite values.
Results may differ from the reference program's by a relative error of at most 0.013.
Values may be sent and summed in bfloat16 or wider, within the bound.
A program may use at most 128 MiB of HBM per device.

```python
import math
import jax
import jax.numpy as jnp
import numpy as np
from jax import lax

E = 256
H = 1024
FEAT = 512
Q_DEV = 1024
QUERIES = 32768
ITEMS = 512


def draw_query_features(key, part):
    key_base = jax.random.fold_in(key, 11)
    values = jax.random.truncated_normal(key_base, -6.0, 6.0, (QUERIES, FEAT), jnp.float32)
    return values.astype(jnp.bfloat16)


def draw_query_weights(key, part):
    key_spread = jax.random.fold_in(key, 21)
    position = jnp.arange(QUERIES, dtype=jnp.float32) / (QUERIES - 1)
    spread = jnp.exp(jax.random.uniform(key_spread, (QUERIES,), jnp.float32, math.log(0.5), math.log(1.5)))
    return (spread * (1.0 + 2.0 * position)).astype(jnp.bfloat16)


def with_ends(array, rng, low, high):
    index_at = [jax.random.randint(jax.random.fold_in(rng, axis), (), 0, length) for axis, length in enumerate(array.shape)]
    main_axis = array.shape.index(max(array.shape))
    beside = index_at[:main_axis] + [(index_at[main_axis] + 1) % array.shape[main_axis]] + index_at[main_axis + 1:]
    return array.at[tuple(index_at)].set(low).at[tuple(beside)].set(high)


def shard_levels(key, shape, split, low, largest):
    def one(dim, parts):
        steps = jax.random.uniform(jax.random.fold_in(jax.random.fold_in(key, 6), dim), (parts,), jnp.float32, low / len(split), largest / len(split))
        return jnp.repeat(jnp.exp(steps), shape[dim] // parts).reshape((-1,) + (1,) * (len(shape) - dim - 1))

    level = one(*split[0])
    for cut in split[1:]:
        level = level * one(*cut)
    return level


def rank_bounds(count, lean):
    loads = [(1 << 20) // math.isqrt(rank ** lean) + 1 for rank in range(1, count + 1)]
    deviation = 1 + sum(loads) // (1 << 30)
    return np.cumsum(np.array([max(1, weight // deviation) for weight in loads]))


def ranked_ids(own_key, shape, amount, lean):
    grid = rank_bounds(amount, lean)
    lot = jax.random.randint(jax.random.fold_in(own_key, 1), shape, 0, int(grid[amount - 1]))
    rank = jnp.searchsorted(jnp.asarray(grid, jnp.int32), lot, side="right")
    return jax.random.permutation(jax.random.fold_in(own_key, 2), amount)[rank].astype(jnp.int32)


def gaussian(key, shape, width, limit, split=(), held_as=jnp.bfloat16):
    result = jax.random.normal(key, shape, jnp.float32) * width
    if len(split) > 0:
        result = shard_levels(key, shape, split, -0.22, 0.18) * result
    return jnp.clip(result, min=-limit, max=limit).astype(held_as)


def setup_inputs(seed: int = 0) -> dict:
    streams_of = jax.random.split(jax.random.key(seed), 11)
    query_features = draw_query_features(jax.random.fold_in(streams_of[10], 71), 0)
    query_weights = draw_query_weights(jax.random.fold_in(streams_of[10], 71), 0)
    positive_index = with_ends(jax.random.randint(streams_of[2], (QUERIES,), 0, ITEMS), jax.random.fold_in(streams_of[2], 1), 0, ITEMS - 1).astype(jnp.int32)
    item_features = gaussian(streams_of[3], (ITEMS, FEAT), 1.0, 6.0, ((0, 32),))
    item_ids = with_ends(ranked_ids(streams_of[4], (ITEMS,), ITEMS // 2, 2), jax.random.fold_in(streams_of[4], 3), 0, (ITEMS // 2) - 1).astype(jnp.int32)
    item_logq = jnp.clip(-14.0 + 3.0 * jax.random.uniform(streams_of[5], (ITEMS,), jnp.float32) ** shard_levels(streams_of[5], (ITEMS,), ((0, 32),), -0.2, 0.2), -14.0, -11.0).astype(jnp.bfloat16)
    query_w_in = gaussian(streams_of[6], (FEAT, H), FEAT ** -0.5, 0.25)
    query_w_out = gaussian(streams_of[7], (H, E), H ** -0.5, 0.1875)
    item_w_in = gaussian(streams_of[8], (FEAT, H), FEAT ** -0.5, 0.25)
    item_w_out = gaussian(streams_of[9], (H, E), H ** -0.5, 0.1875)
    return {"query_features": query_features, "query_weights": query_weights, "positive_index": positive_index, "item_features": item_features, "item_ids": item_ids, "item_logq": item_logq, "query_w_in": query_w_in, "query_w_out": query_w_out, "item_w_in": item_w_in, "item_w_out": item_w_out}


score_scale = 0.25
loss_scale = 1024.0


def silu_slope(values):
    gate = jax.nn.sigmoid(values)
    return gate * (1.0 + values * (1.0 - gate))


def tower(features, weight_in, weight_out):
    pre_act = jnp.dot(features, weight_in, preferred_element_type=jnp.float32)
    hidden = jax.nn.silu(pre_act).astype(jnp.bfloat16)
    embedding = jnp.dot(hidden, weight_out, preferred_element_type=jnp.float32).astype(jnp.bfloat16)
    return pre_act, hidden, embedding


def tower_back(features, pre_act, hidden, weight_out, embed_grad):
    grad_out = jnp.dot(hidden.T, embed_grad, preferred_element_type=jnp.float32)
    hidden_grad = jnp.dot(embed_grad, weight_out.T, preferred_element_type=jnp.float32)
    pre_grad = (hidden_grad * silu_slope(pre_act)).astype(jnp.bfloat16)
    grad_in = jnp.dot(features.T, pre_grad, preferred_element_type=jnp.float32)
    return grad_in, grad_out


def item_scores(query_rows, items, item_bias, item_codes, columns, positives, pos_codes):
    raw_scores = lax.dot_general(query_rows, items, (((1,), (1,)), ((), ())), preferred_element_type=jnp.float32)
    scores = score_scale * raw_scores - item_bias[None, :]
    masked_hits = (item_codes[None, :] == pos_codes[:, None]) & (columns[None, :] != positives[:, None])
    return jnp.where(masked_hits, -jnp.inf, scores)


def partial_stats(scores):
    row_max = jnp.maximum(jnp.max(scores, axis=1), -1e30)
    row_sum = jnp.sum(jnp.exp(scores - row_max[:, None]), axis=1)
    return row_max, row_sum


def finish(scores, row_max, row_sum, columns, positives, weights):
    probability = jnp.exp(scores - row_max[:, None]) / row_sum[:, None]
    target = (columns[None, :] == positives[:, None]).astype(jnp.float32)
    return (weights.astype(jnp.float32)[:, None] * (probability - target)).astype(jnp.bfloat16)


def reference(query_features, query_weights, positive_index, item_features, item_ids, item_logq, query_w_in, query_w_out, item_w_in, item_w_out):
    item_pre, item_hidden, item_embed = tower(item_features, item_w_in, item_w_out)
    item_columns = jnp.arange(ITEMS, dtype=jnp.int32)
    item_bias = item_logq.astype(jnp.float32)

    def one_block(running, block_index):
        first_row = (block_index * Q_DEV).astype(jnp.int32)
        features = lax.dynamic_slice_in_dim(query_features, first_row, Q_DEV, 0)
        weights = lax.dynamic_slice_in_dim(query_weights, first_row, Q_DEV, 0)
        positives = lax.dynamic_slice_in_dim(positive_index, first_row, Q_DEV, 0)
        query_pre, query_hidden, query_embed = tower(features, query_w_in, query_w_out)
        pos_codes = jnp.take(item_ids, positives)
        scores = item_scores(query_embed, item_embed, item_bias, item_ids, item_columns, positives, pos_codes)
        row_max, row_sum = partial_stats(scores)
        dlogit = finish(scores, row_max, row_sum, item_columns, positives, weights)
        query_grad = (score_scale * jnp.dot(dlogit, item_embed, preferred_element_type=jnp.float32)).astype(jnp.bfloat16)
        grad_in, grad_out = tower_back(features, query_pre, query_hidden, query_w_out, query_grad)
        item_term = score_scale * lax.dot_general(dlogit, query_embed, (((0,), (0,)), ((), ())), preferred_element_type=jnp.float32)
        return (running[0] + item_term, running[1] + grad_in, running[2] + grad_out), None

    initial = (jnp.zeros((ITEMS, E), jnp.float32), jnp.zeros((FEAT, H), jnp.float32), jnp.zeros((H, E), jnp.float32))
    (item_sum, query_in_sum, query_out_sum), unused = lax.scan(one_block, initial, jnp.arange(QUERIES // Q_DEV, dtype=jnp.int32))
    item_grad = item_sum.astype(jnp.bfloat16)
    item_in_sum, item_out_sum = tower_back(item_features, item_pre, item_hidden, item_w_out, item_grad)
    factor = loss_scale / jnp.sum(query_weights.astype(jnp.float32))
    return (query_in_sum * factor, query_out_sum * factor, item_in_sum * factor, item_out_sum * factor)
```

```python
import functools

import jax
import jax.numpy as jnp
from jax import lax
from jax.experimental import pallas as pl
from jax.experimental.pallas import tpu as pltpu
from jax.sharding import PartitionSpec as P

MESH = pl.DeviceIdType.MESH
F32 = jnp.float32
BF16 = jnp.bfloat16
SCALE = 0.25
LOSS = 1024.0
NN = (((1,), (0,)), ((), ()))
NT = (((1,), (1,)), ((), ()))
TN = (((0,), (0,)), ((), ()))


def dot(a, b, dims=NN):
    return lax.dot_general(a, b, dims, preferred_element_type=F32)


def gate_of(v):
    return 1.0 / (1.0 + jnp.exp(-v))


def kernel(
    D, k, QT, AT, CW, PR,
    qf, qw, pos, feat, ids, logq, wqi, wqo, wii, wio,
    oqi, oqo, oii, oio, ofac,
    feats, meta, slope, hid, hidT, qfT, qemb, qgrad, iemb, igrad, buf, rcv, gat,
    ag_send, ag_recv, mt_send, mt_recv, pair_send, pair_recv,
    rs_send, rs_recv, fg_send, fg_recv,
):
    dp = lax.axis_index("dp")
    grp = lax.axis_index("grp")
    Q, FE = qf.shape
    H, E = wqo.shape
    NI = feat.shape[0]
    I = D * 2 * NI
    other = 1 - grp
    n_item = I // PR
    n_out = H // PR
    n_in = H // CW
    parts = n_item + n_out + n_in

    barrier = pltpu.get_barrier_semaphore()

    def greet(o, c):
        pl.semaphore_signal(barrier, inc=1, device_id=(lax.rem(dp + o, D), grp), device_id_type=MESH)
        return c

    lax.fori_loop(1, D, greet, 0)
    pl.semaphore_signal(barrier, inc=1, device_id=(dp, other), device_id_type=MESH)

    feats[dp, grp] = feat[...]
    eye = lax.broadcasted_iota(jnp.int32, (NI, NI), 0) == lax.broadcasted_iota(jnp.int32, (NI, NI), 1)
    id_col = jnp.sum(jnp.where(eye, ids[...].astype(F32), 0.0), axis=1, keepdims=True)
    lq_col = jnp.sum(jnp.where(eye, logq[...].astype(F32), 0.0), axis=1, keepdims=True)
    w_sum = jnp.sum(qw[...].astype(F32), axis=1, keepdims=True)
    lane = lax.broadcasted_iota(jnp.int32, (NI, 128), 1)
    meta[dp, grp] = jnp.where(lane == 0, id_col, jnp.where(lane == 1, lq_col, jnp.where(lane == 2, w_sum, 0.0)))

    pl.semaphore_wait(barrier, D)

    def ag_copies(o):
        to = (lax.rem(dp + o, D), grp)
        a = pltpu.make_async_remote_copy(
            src_ref=feat, dst_ref=feats.at[dp, grp], send_sem=ag_send.at[o], recv_sem=ag_recv.at[o],
            device_id=to, device_id_type=MESH)
        b = pltpu.make_async_remote_copy(
            src_ref=meta.at[dp, grp], dst_ref=meta.at[dp, grp], send_sem=mt_send.at[o], recv_sem=mt_recv.at[o],
            device_id=to, device_id_type=MESH)
        return a, b

    def ag_start(o, c):
        a, b = ag_copies(o)
        a.start()
        b.start()
        return c

    lax.fori_loop(1, D, ag_start, 0)

    def forward(t, c):
        rows = pl.ds(pl.multiple_of(t * QT, QT), QT)
        pre = dot(qf[rows, :], wqi[...])
        g = gate_of(pre)
        h = (pre * g).astype(BF16)
        slope[rows, :] = g * (1.0 + pre * (1.0 - g))
        hid[rows, :] = h
        qemb[rows, :] = dot(h, wqo[...]).astype(BF16)
        return c

    lax.fori_loop(0, Q // QT, forward, 0)
    hidT[...] = hid[...].T
    qfT[...] = qf[...].T

    def ag_wait(o, c):
        a, b = ag_copies(o)
        a.wait()
        b.wait()
        return c

    lax.fori_loop(1, D, ag_wait, 0)

    pair = (dp, other)
    pf = pltpu.make_async_remote_copy(
        src_ref=feats.at[:, grp], dst_ref=feats.at[:, grp], send_sem=pair_send.at[0], recv_sem=pair_recv.at[0],
        device_id=pair, device_id_type=MESH)
    pm = pltpu.make_async_remote_copy(
        src_ref=meta.at[:, grp], dst_ref=meta.at[:, grp], send_sem=pair_send.at[1], recv_sem=pair_recv.at[1],
        device_id=pair, device_id_type=MESH)
    pf.start()
    pm.start()
    pf.wait()
    pm.wait()

    for r in range(n_item):
        blk = D // n_item
        x = feats[r * blk:(r + 1) * blk].reshape(PR, FE)
        pre = dot(x, wii[...])
        h = (pre * gate_of(pre)).astype(BF16)
        iemb[r * PR:(r + 1) * PR, :] = dot(h, wio[...]).astype(BF16)

    info = meta[...].reshape(I, 128)
    id_all = info[:, 0:1]
    lq_all = info[:, 1:2]
    total = jnp.sum(info[:, 2:3], axis=0, keepdims=True) * (1.0 / NI)
    factor = LOSS / total
    ofac[...] = jnp.broadcast_to(factor, ofac.shape)

    def attend(t, c):
        rows = pl.ds(pl.multiple_of(t * AT, AT), AT)
        e_t = qemb[rows, :]
        s = SCALE * dot(iemb[...], e_t, NT) - lq_all
        hit = lax.broadcasted_iota(jnp.int32, (I, AT), 0) == pos[:, rows]
        pid = jnp.sum(jnp.where(hit, id_all, 0.0), axis=0, keepdims=True)
        s = jnp.where(jnp.logical_and(id_all == pid, jnp.logical_not(hit)), -jnp.inf, s)
        m = jnp.maximum(jnp.max(s, axis=0, keepdims=True), -1e30)
        ex = jnp.exp(s - m)
        inv = 1.0 / jnp.sum(ex, axis=0, keepdims=True)
        w = qw[:, rows].astype(F32)
        d = (w * (ex * inv - jnp.where(hit, 1.0, 0.0))).astype(BF16)
        term = dot(d, e_t)
        igrad[...] = jnp.where(t == 0, term, igrad[...] + term)
        qgrad[rows, :] = (SCALE * dot(d, iemb[...], TN)).astype(BF16)
        return c

    igrad[...] = jnp.zeros_like(igrad)
    lax.fori_loop(0, Q // AT, attend, 0)

    halves = 0
    while halves < k + 1 and PR >> (halves + 1) >= 16:
        halves += 1
    bits = list(range(k))
    turned = bits[2:] + bits[:2]
    orders = [bits, [bits[1], bits[0]] + bits[2:], turned, bits, [bits[1], bits[0]] + bits[2:], turned[:-2] + [turned[-1], turned[-2]]]

    def peer(bit):
        if bit < 0:
            return grp, (dp, other)
        one = 1 << bit
        mine = lax.rem(lax.div(dp, one), 2)
        return mine, (dp + one * (1 - 2 * mine), grp)

    def plan(p):
        steps, off, rows = [], 0, PR
        slot = 0
        for s, bit in enumerate([-1] + orders[p % 6]):
            mine, to = peer(bit)
            if s < halves:
                rows //= 2
                send, off = off + (1 - mine) * rows, off + mine * rows
                steps.append((True, rows, send, off, slot, to))
            else:
                steps.append((False, rows, off, off, slot, to))
            slot += max(rows, 16)
        return steps

    plans = [plan(p) for p in range(parts)]

    def at(off, rows):
        return pl.ds(pl.multiple_of(off, 16), rows)

    def rs_copy(p, s):
        half, rows, send, keep, slot, to = plans[p][s]
        return pltpu.make_async_remote_copy(
            src_ref=buf.at[p, at(send, rows)],
            dst_ref=rcv.at[p, pl.ds(slot, rows)],
            send_sem=rs_send.at[p, s], recv_sem=rs_recv.at[p, s], device_id=to, device_id_type=MESH)

    def fg_copy(p, s):
        half, rows, send, keep, slot, to = plans[p][s]
        return pltpu.make_async_remote_copy(
            src_ref=gat.at[p, at(keep, rows)], dst_ref=gat.at[p, at(keep, rows)],
            send_sem=fg_send.at[p, s], recv_sem=fg_recv.at[p, s], device_id=to, device_id_type=MESH)

    last = k

    def advance(p, n):
        if n == 0:
            rs_copy(p, 0).start()
        elif n <= last + 1:
            s = n - 1
            rs_copy(p, s).wait()
            half, rows, send, keep, slot, to = plans[p][s]
            got = buf[p, at(keep, rows)].astype(F32) + rcv[p, pl.ds(slot, rows)].astype(F32)
            if s < last:
                buf[p, at(keep, rows)] = got.astype(BF16)
                rs_copy(p, s + 1).start()
            else:
                gat[p, at(keep, rows)] = got.astype(BF16)
                fg_copy(p, halves - 1).start()
        else:
            s = halves - 1 - (n - last - 2)
            fg_copy(p, s).wait()
            if s > 0:
                fg_copy(p, s - 1).start()

    turns = last + 2 + halves
    items = range(n_item)
    outs = range(n_item, n_item + n_out)
    ins = range(n_item + n_out, parts)

    for p in items:
        buf[p] = (SCALE * igrad[p * PR:(p + 1) * PR, :]).astype(BF16)
        advance(p, 0)
    step_i = 1

    g_out = dot(hidT[...], qgrad[...])
    for j, p in enumerate(outs):
        buf[p] = g_out[j * PR:(j + 1) * PR, :].astype(BF16)
        advance(p, 0)
    for p in items:
        advance(p, step_i)
    step_i += 1

    for j, p in enumerate(ins):
        cols = slice(j * CW, (j + 1) * CW)
        hg = dot(qgrad[...], wqo[cols, :], NT)
        pg = (hg * slope[:, cols]).astype(BF16)
        buf[p] = dot(qfT[...], pg).astype(BF16)
        advance(p, 0)
        for q in items:
            advance(q, step_i)
        step_i += 1

    def item_back(j):
        cols = slice(j * CW, (j + 1) * CW)
        x = feats[...].reshape(I, FE)
        ig = gat[0:n_item].reshape(I, E)
        pre = dot(x, wii[:, cols])
        g = gate_of(pre)
        h = (pre * g).astype(BF16)
        oio[cols, :] = dot(h, ig, TN)
        hg = dot(ig, wio[cols, :], NT)
        pg = (hg * (g * (1.0 + pre * (1.0 - g)))).astype(BF16)
        oii[:, cols] = dot(x, pg, TN)

    done = 0
    for n in range(1, turns):
        for p in list(outs) + list(ins):
            advance(p, n)
        for _ in range(2):
            if step_i < turns:
                for q in items:
                    advance(q, step_i)
                step_i += 1
        if step_i >= turns and done < n_in:
            item_back(done)
            done += 1
    while done < n_in:
        item_back(done)
        done += 1

    for j, p in enumerate(outs):
        oqo[j * PR:(j + 1) * PR, :] = gat[p]
    for j, p in enumerate(ins):
        oqi[:, j * CW:(j + 1) * CW] = gat[p]


def solution(mesh):
    D = mesh.shape["dp"]
    k = D.bit_length() - 1

    def on_device(qf, qw, pos, feat, ids, logq, wqi, wqo, wii, wio):
        Q, FE = qf.shape
        H, E = wqo.shape
        NI = feat.shape[0]
        I = NI * D * 2
        QT, CW, PR = 256, E, FE
        AT = QT if I <= 4 * QT else QT // 2
        parts = I // PR + H // PR + H // CW
        vm = pl.BlockSpec(memory_space=pltpu.VMEM)
        dma = pltpu.SemaphoreType.DMA
        oqi, oqo, oii, oio, fac = pl.pallas_call(
            functools.partial(kernel, D, k, QT, AT, CW, PR),
            name="retrieval_grads",
            out_shape=(
                jax.ShapeDtypeStruct((FE, H), BF16),
                jax.ShapeDtypeStruct((H, E), BF16),
                jax.ShapeDtypeStruct((FE, H), F32),
                jax.ShapeDtypeStruct((H, E), F32),
                jax.ShapeDtypeStruct((8, 128), F32),
            ),
            in_specs=[vm] * 10,
            out_specs=(vm,) * 5,
            scratch_shapes=[
                pltpu.VMEM((D, 2, NI, FE), BF16),
                pltpu.VMEM((D, 2, NI, 128), F32),
                pltpu.VMEM((Q, H), F32),
                pltpu.VMEM((Q, H), BF16),
                pltpu.VMEM((H, Q), BF16),
                pltpu.VMEM((FE, Q), BF16),
                pltpu.VMEM((Q, E), BF16),
                pltpu.VMEM((Q, E), BF16),
                pltpu.VMEM((I, E), BF16),
                pltpu.VMEM((I, E), F32),
                pltpu.VMEM((parts, PR, E), BF16),
                pltpu.VMEM((parts, PR + 64, E), BF16),
                pltpu.VMEM((parts, PR, E), BF16),
                dma((D,)), dma((D,)), dma((D,)), dma((D,)), dma((2,)), dma((2,)),
                dma((parts, k + 1)), dma((parts, k + 1)), dma((parts, k + 1)), dma((parts, k + 1)),
            ],
            compiler_params=pltpu.CompilerParams(
                collective_id=0, has_side_effects=True, vmem_limit_bytes=(48 if I <= 4 * QT else 62) * 1024 * 1024),
        )(qf, qw.reshape(1, Q), pos.reshape(1, Q), feat, ids.reshape(1, NI), logq.reshape(1, NI), wqi, wqo, wii, wio)
        f = fac[0, 0]
        return (oqi.astype(F32) * f, oqo.astype(F32) * f, oii * f, oio * f)

    rows = P(("dp", "grp"), None)
    flat = P(("dp", "grp"))
    return jax.shard_map(
        on_device, mesh=mesh,
        in_specs=(rows, flat, flat, rows, flat, flat, P(), P(), P(), P()),
        out_specs=(P(), P(), P(), P()),
        check_vma=False,
    )
```

```python
import functools

import jax
import jax.numpy as jnp
from jax import lax
from jax.experimental import pallas as pl
from jax.experimental.pallas import tpu as pltpu
from jax.sharding import PartitionSpec as P

MESH = pl.DeviceIdType.MESH
F32 = jnp.float32
BF16 = jnp.bfloat16
SCALE = 0.25
LOSS = 1024.0
NN = (((1,), (0,)), ((), ()))
NT = (((1,), (1,)), ((), ()))
TN = (((0,), (0,)), ((), ()))


def dot(a, b, dims=NN):
    return lax.dot_general(a, b, dims, preferred_element_type=F32)


def gate_of(v):
    return 1.0 / (1.0 + jnp.exp(-v))


def kernel(
    D, k, QT, AT, CW, PR,
    qf_h, qw_h, pos_h, feat_h, ids_h, logq_h, wqi_h, wqo_h, wii_h, wio_h,
    oqi, oqo, oii, oio, ofac,
    qf, qw, pos, ids, logq, wqi, wqo, wii, wio, load,
    feats, meta, embs, slope, hid, hidT, qfT, qemb, qgrad, igrad, buf, rcv, gat,
    em_send, em_recv, ag_send, ag_recv, mt_send, mt_recv, pair_send, pair_recv,
    rs_send, rs_recv, fg_send, fg_recv,
):
    dp = lax.axis_index("dp")
    grp = lax.axis_index("grp")
    Q, FE = qf.shape
    H, E = wqo.shape
    NI = feat_h.shape[0]
    I = D * 2 * NI
    other = 1 - grp
    n_item = I // PR
    n_out = H // PR
    n_in = H // CW
    parts = n_item + n_out + n_in

    mine_at = feats.at[dp, grp]
    pairs = [(feat_h, mine_at), (wii_h, wii), (wio_h, wio), (ids_h, ids), (logq_h, logq), (qw_h, qw), (wqi_h, wqi),
             (qf_h, qf), (wqo_h, wqo), (pos_h, pos)]
    loads = [pltpu.make_async_copy(a, b, load.at[i]) for i, (a, b) in enumerate(pairs)]
    for c in loads:
        c.start()

    barrier = pltpu.get_barrier_semaphore()

    def greet(o, c):
        pl.semaphore_signal(barrier, inc=1, device_id=(lax.rem(dp + o, D), grp), device_id_type=MESH)
        return c

    lax.fori_loop(1, D, greet, 0)
    pl.semaphore_signal(barrier, inc=1, device_id=(dp, other), device_id_type=MESH)

    for c in loads[:6]:
        c.wait()
    i_pre = dot(mine_at[...], wii[...])
    embs[dp, grp] = dot((i_pre * gate_of(i_pre)).astype(BF16), wio[...]).astype(BF16)
    meta[dp, grp] = jnp.zeros((8, 128), F32)
    meta[dp, grp, 0:1, 0:NI] = ids[...].astype(F32)
    meta[dp, grp, 1:2, 0:NI] = logq[...].astype(F32)
    meta[dp, grp, 2:3, :] = jnp.broadcast_to(jnp.sum(qw[...].astype(F32), axis=1, keepdims=True), (1, 128))

    pl.semaphore_wait(barrier, D)

    def to_all(ref, send, recv):
        def copy(o):
            return pltpu.make_async_remote_copy(
                src_ref=ref.at[dp, grp], dst_ref=ref.at[dp, grp], send_sem=send.at[o], recv_sem=recv.at[o],
                device_id=(lax.rem(dp + o, D), grp), device_id_type=MESH)

        def start(o, c):
            copy(o).start()
            return c

        def wait(o, c):
            copy(o).wait()
            return c

        return (lambda: lax.fori_loop(1, D, start, 0)), (lambda: lax.fori_loop(1, D, wait, 0))

    def to_pair(ref, i):
        return pltpu.make_async_remote_copy(
            src_ref=ref.at[:, grp], dst_ref=ref.at[:, grp], send_sem=pair_send.at[i], recv_sem=pair_recv.at[i],
            device_id=(dp, other), device_id_type=MESH)

    emb_start, emb_wait = to_all(embs, em_send, em_recv)
    meta_start, meta_wait = to_all(meta, mt_send, mt_recv)
    feat_start, feat_wait = to_all(feats, ag_send, ag_recv)
    meta_start()
    emb_start()
    feat_start()

    for c in loads[6:9]:
        c.wait()

    def forward(t, c):
        rows = pl.ds(pl.multiple_of(t * QT, QT), QT)
        pre = dot(qf[rows, :], wqi[...])
        g = gate_of(pre)
        h = (pre * g).astype(BF16)
        slope[rows, :] = g * (1.0 + pre * (1.0 - g))
        hid[rows, :] = h
        qemb[rows, :] = dot(h, wqo[...]).astype(BF16)
        return c

    lax.fori_loop(0, Q // QT, forward, 0)
    hidT[...] = hid[...].T
    qfT[...] = qf[...].T

    loads[9].wait()
    meta_wait()
    pm = to_pair(meta, 0)
    pm.start()
    emb_wait()
    pe = to_pair(embs, 1)
    pe.start()
    pm.wait()
    pe.wait()

    diag = lax.broadcasted_iota(jnp.int32, (1, NI, 128), 1) == lax.broadcasted_iota(jnp.int32, (1, NI, 128), 2)

    def column(r):
        row = meta[:, :, r:r + 1, :].reshape(2 * D, 1, 128)
        return jnp.sum(jnp.where(diag, row, 0.0), axis=2, keepdims=True).reshape(I, 1)

    id_all = column(0)
    lq_all = column(1)
    total = jnp.sum(meta[:, :, 2:3, :].reshape(2 * D, 128)[:, 0:1], axis=0, keepdims=True)
    factor = LOSS / total
    ofac[...] = jnp.broadcast_to(factor, ofac.shape)

    def attend(t, c):
        rows = pl.ds(pl.multiple_of(t * AT, AT), AT)
        e_t = qemb[rows, :]
        i_emb = embs[...].reshape(I, E)
        s = SCALE * dot(i_emb, e_t, NT) - lq_all
        hit = lax.broadcasted_iota(jnp.int32, (I, AT), 0) == pos[:, rows]
        pid = jnp.sum(jnp.where(hit, id_all, 0.0), axis=0, keepdims=True)
        s = jnp.where(jnp.logical_and(id_all == pid, jnp.logical_not(hit)), -jnp.inf, s)
        m = jnp.maximum(jnp.max(s, axis=0, keepdims=True), -1e30)
        ex = jnp.exp(s - m)
        inv = 1.0 / jnp.sum(ex, axis=0, keepdims=True)
        w = qw[:, rows].astype(F32)
        d = (w * (ex * inv - jnp.where(hit, 1.0, 0.0))).astype(BF16)
        term = dot(d, e_t)
        igrad[...] = jnp.where(t == 0, term, igrad[...] + term)
        qgrad[rows, :] = (SCALE * dot(d, i_emb, TN)).astype(BF16)
        return c

    igrad[...] = jnp.zeros_like(igrad)
    lax.fori_loop(0, Q // AT, attend, 0)

    bits = list(range(k))
    tail = [[2, 3]] + [[b] for b in bits[4:]] if k >= 4 else [[b] for b in bits[2:]]
    heads = [[[b] for b in bits[:2]], [[b] for b in bits[:2][::-1]]]

    def plan(p):
        steps, off, rows, slot, sem = [], 0, PR, 0, 0
        for group in [None] + heads[p % 2] + tail:
            ways = 2 if group is None else 1 << len(group)
            one = 1 if group is None else 1 << group[0]
            digit = grp if group is None else lax.rem(lax.div(dp, one), ways)
            split = rows // ways >= 16
            size = rows // ways if split else rows
            moves = []
            for o in range(1, ways):
                there = lax.rem(digit + o, ways)
                to = (dp, there) if group is None else (dp + one * (there - digit), grp)
                moves.append((to, off + there * size if split else off, slot, sem))
                slot += size
                sem += 1
            off = off + digit * size if split else off
            rows = size
            steps.append((split, size, off, moves))
        return steps

    plans = [plan(p) for p in range(parts)]
    stages = len(plans[0])
    back = [s for s in range(stages) if plans[0][s][0]][::-1]
    turns = 1 + stages + len(back)

    def at(off, rows):
        return pl.ds(pl.multiple_of(off, 16), rows)

    def out_copies(p, s):
        split, size, keep, moves = plans[p][s]
        return [pltpu.make_async_remote_copy(
            src_ref=buf.at[p, at(send, size)], dst_ref=rcv.at[p, pl.ds(slot, size)],
            send_sem=rs_send.at[p, i], recv_sem=rs_recv.at[p, i], device_id=to, device_id_type=MESH)
            for to, send, slot, i in moves]

    def back_copies(p, s):
        split, size, keep, moves = plans[p][s]
        return [pltpu.make_async_remote_copy(
            src_ref=gat.at[p, at(keep, size)], dst_ref=gat.at[p, at(keep, size)],
            send_sem=fg_send.at[p, i], recv_sem=fg_recv.at[p, i], device_id=to, device_id_type=MESH)
            for to, send, slot, i in moves]

    def start(copies):
        for c in copies:
            c.start()

    def wait(copies):
        for c in copies:
            c.wait()

    def advance(p, n):
        if n == 0:
            start(out_copies(p, 0))
        elif n <= stages:
            s = n - 1
            wait(out_copies(p, s))
            split, size, keep, moves = plans[p][s]
            got = buf[p, at(keep, size)].astype(F32)
            for to, send, slot, i in moves:
                got = got + rcv[p, pl.ds(slot, size)].astype(F32)
            if n < stages:
                buf[p, at(keep, size)] = got.astype(BF16)
                start(out_copies(p, n))
            else:
                gat[p, at(keep, size)] = got.astype(BF16)
                start(back_copies(p, back[0]))
        else:
            i = n - stages - 1
            wait(back_copies(p, back[i]))
            if i + 1 < len(back):
                start(back_copies(p, back[i + 1]))
            elif p in outs:
                oqo[(p - outs[0]) * PR:(p - outs[0] + 1) * PR, :] = gat[p]
            elif p in ins:
                oqi[:, (p - ins[0]) * CW:(p - ins[0] + 1) * CW] = gat[p]

    items = range(n_item)
    outs = range(n_item, n_item + n_out)
    ins = range(n_item + n_out, parts)

    for p in items:
        buf[p] = (SCALE * igrad[p * PR:(p + 1) * PR, :]).astype(BF16)
        advance(p, 0)

    g_out = dot(hidT[...], qgrad[...])
    for j, p in enumerate(outs):
        buf[p] = g_out[j * PR:(j + 1) * PR, :].astype(BF16)
        advance(p, 0)
    for p in items:
        advance(p, 1)

    for j, p in enumerate(ins):
        cols = slice(j * CW, (j + 1) * CW)
        hg = dot(qgrad[...], wqo[cols, :], NT)
        pg = (hg * slope[:, cols]).astype(BF16)
        buf[p] = dot(qfT[...], pg).astype(BF16)
        advance(p, 0)
        if j == 1:
            for q in items:
                advance(q, 2)

    feat_wait()
    pf = to_pair(feats, 2)
    pf.start()
    step_i = 3

    def item_back(j):
        cols = slice(j * CW, (j + 1) * CW)
        x = feats[...].reshape(I, FE)
        ig = gat[0:n_item].reshape(I, E)
        pre = dot(x, wii[:, cols])
        g = gate_of(pre)
        h = (pre * g).astype(BF16)
        oio[cols, :] = dot(h, ig, TN) * factor
        hg = dot(ig, wio[cols, :], NT)
        pg = (hg * (g * (1.0 + pre * (1.0 - g)))).astype(BF16)
        oii[:, cols] = dot(x, pg, TN) * factor

    done = 0
    for n in range(1, turns):
        for p in list(outs) + list(ins):
            advance(p, n)
        if step_i < turns:
            for q in items:
                advance(q, step_i)
            step_i += 1
            if step_i == turns:
                pf.wait()
        elif done < n_in:
            for _ in range(2):
                item_back(done)
                done += 1
    while done < n_in:
        item_back(done)
        done += 1


def finish(qi, qo, ii, io, fac, gqi, gqo, gii, gio, bi, bo, sem):
    direct = [pltpu.make_async_copy(ii, gii, sem.at[0]), pltpu.make_async_copy(io, gio, sem.at[1])]
    for c in direct:
        c.start()
    f = fac[0:1, 0:1]
    bo[...] = qo[...].astype(F32) * f
    a = pltpu.make_async_copy(bo, gqo, sem.at[2])
    a.start()
    bi[...] = qi[...].astype(F32) * f
    b = pltpu.make_async_copy(bi, gqi, sem.at[3])
    b.start()
    for c in direct + [a, b]:
        c.wait()


def solution(mesh):
    D = mesh.shape["dp"]
    k = D.bit_length() - 1

    def on_device(qf, qw, pos, feat, ids, logq, wqi, wqo, wii, wio):
        Q, FE = qf.shape
        H, E = wqo.shape
        NI = feat.shape[0]
        I = NI * D * 2
        QT, CW, PR = 256, E, FE
        AT = QT if I <= 4 * QT else QT // 2
        parts = I // PR + H // PR + H // CW
        vm = pl.BlockSpec(memory_space=pltpu.VMEM)
        dma = pltpu.SemaphoreType.DMA
        args = (qf, qw.reshape(1, Q), pos.reshape(1, Q), feat, ids.reshape(1, NI), logq.reshape(1, NI), wqi, wqo, wii, wio)
        oqi, oqo, oii, oio, fac = pl.pallas_call(
            functools.partial(kernel, D, k, QT, AT, CW, PR),
            name="retrieval_grads",
            out_shape=(
                jax.ShapeDtypeStruct((FE, H), BF16),
                jax.ShapeDtypeStruct((H, E), BF16),
                jax.ShapeDtypeStruct((FE, H), F32),
                jax.ShapeDtypeStruct((H, E), F32),
                jax.ShapeDtypeStruct((8, 128), F32),
            ),
            in_specs=[pl.BlockSpec(memory_space=pltpu.HBM)] * 10,
            out_specs=(vm,) * 5,
            scratch_shapes=[
                pltpu.VMEM((Q, FE), BF16), pltpu.VMEM((1, Q), BF16), pltpu.VMEM((1, Q), jnp.int32),
                pltpu.VMEM((1, NI), jnp.int32), pltpu.VMEM((1, NI), BF16),
                pltpu.VMEM((FE, H), BF16), pltpu.VMEM((H, E), BF16), pltpu.VMEM((FE, H), BF16), pltpu.VMEM((H, E), BF16),
                dma((10,)),
                pltpu.VMEM((D, 2, NI, FE), BF16),
                pltpu.VMEM((D, 2, 8, 128), F32),
                pltpu.VMEM((D, 2, NI, E), BF16),
                pltpu.VMEM((Q, H), F32),
                pltpu.VMEM((Q, H), BF16),
                pltpu.VMEM((H, Q), BF16),
                pltpu.VMEM((FE, Q), BF16),
                pltpu.VMEM((Q, E), BF16),
                pltpu.VMEM((Q, E), BF16),
                pltpu.VMEM((I, E), F32),
                pltpu.VMEM((parts, PR, E), BF16),
                pltpu.VMEM((parts, PR + 64, E), BF16),
                pltpu.VMEM((parts, PR, E), BF16),
                dma((D,)), dma((D,)), dma((D,)), dma((D,)), dma((D,)), dma((D,)), dma((3,)), dma((3,)),
                dma((parts, 2 * k + 2)), dma((parts, 2 * k + 2)), dma((parts, 2 * k + 2)), dma((parts, 2 * k + 2)),
            ],
            compiler_params=pltpu.CompilerParams(
                collective_id=0, has_side_effects=True, vmem_limit_bytes=(48 if I <= 4 * QT else 62) * 1024 * 1024),
        )(*[pltpu.with_memory_space_constraint(v, pltpu.HBM) for v in args])
        hbm = pl.BlockSpec(memory_space=pltpu.HBM)
        return tuple(pl.pallas_call(
            finish,
            name="finish",
            out_shape=(
                jax.ShapeDtypeStruct((FE, H), F32),
                jax.ShapeDtypeStruct((H, E), F32),
                jax.ShapeDtypeStruct((FE, H), F32),
                jax.ShapeDtypeStruct((H, E), F32),
            ),
            in_specs=[vm] * 5,
            out_specs=(hbm,) * 4,
            scratch_shapes=[pltpu.VMEM((FE, H), F32), pltpu.VMEM((H, E), F32), pltpu.SemaphoreType.DMA((4,))],
            compiler_params=pltpu.CompilerParams(vmem_limit_bytes=8 * 1024 * 1024),
        )(oqi, oqo, oii, oio, fac))

    rows = P(("dp", "grp"), None)
    flat = P(("dp", "grp"))
    return jax.shard_map(
        on_device, mesh=mesh,
        in_specs=(rows, flat, flat, rows, flat, flat, P(), P(), P(), P()),
        out_specs=(P(), P(), P(), P()),
        check_vma=False,
    )
```

```python
import functools

import jax
import jax.numpy as jnp
from jax import lax
from jax.experimental import pallas as pl
from jax.experimental.pallas import tpu as pltpu
from jax.sharding import PartitionSpec as P

MESH = pl.DeviceIdType.MESH
F32 = jnp.float32
BF16 = jnp.bfloat16
SCALE = 0.25
LOSS = 1024.0
NN = (((1,), (0,)), ((), ()))
NT = (((1,), (1,)), ((), ()))
TN = (((0,), (0,)), ((), ()))


def dot(a, b, dims=NN):
    return lax.dot_general(a, b, dims, preferred_element_type=F32)


def gate_of(v):
    return 1.0 / (1.0 + jnp.exp(-v))


def kernel(
    D, k, QT, AT, CW, PR,
    qf_h, qw_h, pos_h, feat_h, ids_h, logq_h, wqi_h, wqo_h, wii_h, wio_h,
    oqi, oqo, oii, oio, ofac,
    qf, qw, pos, ids, logq, wqi, wqo, wii, wio, load,
    feats, meta, embs, slope, hid, hidT, qfT, qemb, qgrad, wrow, igrad, buf, rcv, gat,
    em_send, em_recv, ag_send, ag_recv, mt_send, mt_recv, pair_send, pair_recv,
    rs_send, rs_recv, fg_send, fg_recv,
):
    dp = lax.axis_index("dp")
    grp = lax.axis_index("grp")
    Q, FE = qf.shape
    H, E = wqo.shape
    NI = feat_h.shape[0]
    I = D * 2 * NI
    other = 1 - grp
    n_item = I // PR
    n_out = H // PR
    n_in = H // CW
    parts = n_item + n_out + n_in

    mine_at = feats.at[dp, grp]
    pairs = [(feat_h, mine_at), (wii_h, wii), (wio_h, wio), (ids_h, ids), (logq_h, logq), (qw_h, qw), (wqi_h, wqi),
             (qf_h, qf), (wqo_h, wqo), (pos_h, pos)]
    loads = [pltpu.make_async_copy(a, b, load.at[i]) for i, (a, b) in enumerate(pairs)]
    for c in loads:
        c.start()

    barrier = pltpu.get_barrier_semaphore()

    def greet(o, c):
        pl.semaphore_signal(barrier, inc=1, device_id=(lax.rem(dp + o, D), grp), device_id_type=MESH)
        return c

    lax.fori_loop(1, D, greet, 0)
    pl.semaphore_signal(barrier, inc=1, device_id=(dp, other), device_id_type=MESH)

    for c in loads[:6]:
        c.wait()
    wrow[...] = qw[...].astype(F32).reshape(1, Q)
    i_pre = dot(mine_at[...], wii[...])
    embs[dp, grp] = dot((i_pre * gate_of(i_pre)).astype(BF16), wio[...]).astype(BF16)
    meta[dp, grp] = jnp.zeros((8, 128), F32)
    meta[dp, grp, 0:1, 0:NI] = ids[...].astype(F32)
    meta[dp, grp, 1:2, 0:NI] = logq[...].astype(F32)
    meta[dp, grp, 2:3, :] = jnp.broadcast_to(jnp.sum(wrow[...], axis=1, keepdims=True), (1, 128))

    pl.semaphore_wait(barrier, D)

    def to_all(ref, send, recv):
        def copy(o):
            return pltpu.make_async_remote_copy(
                src_ref=ref.at[dp, grp], dst_ref=ref.at[dp, grp], send_sem=send.at[o], recv_sem=recv.at[o],
                device_id=(lax.rem(dp + o, D), grp), device_id_type=MESH)

        def start(o, c):
            copy(o).start()
            return c

        def wait(o, c):
            copy(o).wait()
            return c

        return (lambda: lax.fori_loop(1, D, start, 0)), (lambda: lax.fori_loop(1, D, wait, 0))

    def to_pair(ref, i):
        return pltpu.make_async_remote_copy(
            src_ref=ref.at[:, grp], dst_ref=ref.at[:, grp], send_sem=pair_send.at[i], recv_sem=pair_recv.at[i],
            device_id=(dp, other), device_id_type=MESH)

    emb_start, emb_wait = to_all(embs, em_send, em_recv)
    meta_start, meta_wait = to_all(meta, mt_send, mt_recv)
    feat_start, feat_wait = to_all(feats, ag_send, ag_recv)
    meta_start()
    emb_start()
    feat_start()

    for c in loads[6:9]:
        c.wait()

    def forward(t, c):
        rows = pl.ds(pl.multiple_of(t * QT, QT), QT)
        pre = dot(qf[rows, :], wqi[...])
        g = gate_of(pre)
        h = (pre * g).astype(BF16)
        slope[rows, :] = g * (1.0 + pre * (1.0 - g))
        hid[rows, :] = h
        qemb[rows, :] = dot(h, wqo[...]).astype(BF16)
        return c

    lax.fori_loop(0, Q // QT, forward, 0)
    hidT[...] = hid[...].T
    qfT[...] = qf[...].T

    loads[9].wait()
    meta_wait()
    pm = to_pair(meta, 0)
    pm.start()
    emb_wait()
    pe = to_pair(embs, 1)
    pe.start()
    pm.wait()
    pe.wait()

    diag = lax.broadcasted_iota(jnp.int32, (1, NI, 128), 1) == lax.broadcasted_iota(jnp.int32, (1, NI, 128), 2)

    def column(r):
        row = meta[:, :, r:r + 1, :].reshape(2 * D, 1, 128)
        return jnp.sum(jnp.where(diag, row, 0.0), axis=2, keepdims=True).reshape(I, 1)

    id_all = column(0)
    lq_all = column(1)
    total = jnp.sum(meta[:, :, 2:3, :].reshape(2 * D, 128)[:, 0:1], axis=0, keepdims=True)
    factor = LOSS / total
    ofac[...] = jnp.broadcast_to(factor, ofac.shape)

    def attend(t, c):
        rows = pl.ds(pl.multiple_of(t * AT, AT), AT)
        e_t = qemb[rows, :]
        i_emb = embs[...].reshape(I, E)
        s = SCALE * dot(i_emb, e_t, NT) - lq_all
        hit = lax.broadcasted_iota(jnp.int32, (I, AT), 0) == pos[:, rows]
        pid = jnp.sum(jnp.where(hit, id_all, 0.0), axis=0, keepdims=True)
        s = jnp.where(jnp.logical_and(id_all == pid, jnp.logical_not(hit)), -jnp.inf, s)
        m = jnp.maximum(jnp.max(s, axis=0, keepdims=True), -1e30)
        ex = jnp.exp(s - m)
        inv = 1.0 / jnp.sum(ex, axis=0, keepdims=True)
        w = wrow[:, rows]
        d = (w * (ex * inv - jnp.where(hit, 1.0, 0.0))).astype(BF16)
        term = dot(d, e_t)
        igrad[...] = jnp.where(t == 0, term, igrad[...] + term)
        qgrad[rows, :] = (SCALE * dot(d, i_emb, TN)).astype(BF16)
        return c

    igrad[...] = jnp.zeros_like(igrad)
    lax.fori_loop(0, Q // AT, attend, 0)

    bits = list(range(k))
    near = [[b] for b in bits[:2]]
    far = [bits[2:4]] if k >= 4 else [[b] for b in bits[2:4]]
    rest = [[b] for b in bits[4:]]

    def order(p):
        if p == n_item:
            return far + near + rest
        return (near if p % 2 == 0 else near[::-1]) + far + rest

    def plan(p):
        steps, off, rows, slot, sem = [], 0, PR, 0, 0
        for group in [None] + order(p):
            ways = 2 if group is None else 1 << len(group)
            one = 1 if group is None else 1 << group[0]
            digit = grp if group is None else lax.rem(lax.div(dp, one), ways)
            split = rows // ways >= 16
            size = rows // ways if split else rows
            moves = []
            for o in range(1, ways):
                there = lax.rem(digit + o, ways)
                to = (dp, there) if group is None else (dp + one * (there - digit), grp)
                moves.append((to, off + there * size if split else off, slot, sem))
                slot += size
                sem += 1
            off = off + digit * size if split else off
            rows = size
            steps.append((split, size, off, moves))
        return steps

    plans = [plan(p) for p in range(parts)]
    stages = len(plans[0])
    back = [s for s in range(stages) if plans[0][s][0]][::-1]
    turns = 1 + stages + len(back)

    def at(off, rows):
        return pl.ds(pl.multiple_of(off, 16), rows)

    def out_copies(p, s):
        split, size, keep, moves = plans[p][s]
        return [pltpu.make_async_remote_copy(
            src_ref=buf.at[p, at(send, size)], dst_ref=rcv.at[p, pl.ds(slot, size)],
            send_sem=rs_send.at[p, i], recv_sem=rs_recv.at[p, i], device_id=to, device_id_type=MESH)
            for to, send, slot, i in moves]

    def back_copies(p, s):
        split, size, keep, moves = plans[p][s]
        return [pltpu.make_async_remote_copy(
            src_ref=gat.at[p, at(keep, size)], dst_ref=gat.at[p, at(keep, size)],
            send_sem=fg_send.at[p, i], recv_sem=fg_recv.at[p, i], device_id=to, device_id_type=MESH)
            for to, send, slot, i in moves]

    def start(copies):
        for c in copies:
            c.start()

    def wait(copies):
        for c in copies:
            c.wait()

    def advance(p, n):
        if n == 0:
            start(out_copies(p, 0))
        elif n <= stages:
            s = n - 1
            wait(out_copies(p, s))
            split, size, keep, moves = plans[p][s]
            got = buf[p, at(keep, size)].astype(F32)
            for to, send, slot, i in moves:
                got = got + rcv[p, pl.ds(slot, size)].astype(F32)
            if n < stages:
                buf[p, at(keep, size)] = got.astype(BF16)
                start(out_copies(p, n))
            else:
                gat[p, at(keep, size)] = got.astype(BF16)
                start(back_copies(p, back[0]))
        else:
            i = n - stages - 1
            wait(back_copies(p, back[i]))
            if i + 1 < len(back):
                start(back_copies(p, back[i + 1]))
            elif p in outs:
                oqo[(p - outs[0]) * PR:(p - outs[0] + 1) * PR, :] = gat[p]
            elif p in ins:
                oqi[:, (p - ins[0]) * CW:(p - ins[0] + 1) * CW] = gat[p]

    items = range(n_item)
    outs = range(n_item, n_item + n_out)
    ins = range(n_item + n_out, parts)

    reached = [0] * parts

    def step(group):
        for p in group:
            if reached[p] < turns:
                advance(p, reached[p])
                reached[p] += 1

    for p in items:
        buf[p] = (SCALE * igrad[p * PR:(p + 1) * PR, :]).astype(BF16)
    step(items)

    g_out = dot(hidT[...], qgrad[...])
    for j, p in enumerate(outs):
        buf[p] = g_out[j * PR:(j + 1) * PR, :].astype(BF16)
    step(outs)
    step(items)

    for j, p in enumerate(ins):
        cols = slice(j * CW, (j + 1) * CW)
        hg = dot(qgrad[...], wqo[cols, :], NT)
        pg = (hg * slope[:, cols]).astype(BF16)
        buf[p] = dot(qfT[...], pg).astype(BF16)
        step([p])
        if j == 0:
            step(outs)
        else:
            step([p - 1])
        if j == 1:
            step(items)

    feat_wait()
    pf = to_pair(feats, 2)
    pf.start()

    def item_back(j):
        cols = slice(j * CW, (j + 1) * CW)
        x = feats[...].reshape(I, FE)
        ig = gat[0:n_item].reshape(I, E)
        pre = dot(x, wii[:, cols])
        g = gate_of(pre)
        h = (pre * g).astype(BF16)
        oio[cols, :] = dot(h, ig, TN) * factor
        hg = dot(ig, wio[cols, :], NT)
        pg = (hg * (g * (1.0 + pre * (1.0 - g)))).astype(BF16)
        oii[:, cols] = dot(x, pg, TN) * factor

    done = 0
    landed = False
    query = list(outs) + list(ins)
    while min(reached) < turns:
        before = max(reached[p] for p in items) < turns
        step(items)
        step(query[:len(query) // 2])
        step(items)
        step(query[len(query) // 2:])
        if not before and done < n_in:
            if not landed:
                pf.wait()
                landed = True
            item_back(done)
            done += 1
    if not landed:
        pf.wait()
    while done < n_in:
        item_back(done)
        done += 1


def finish(qi, qo, ii, io, fac, gqi, gqo, gii, gio, bi, bo, sem):
    direct = [pltpu.make_async_copy(ii, gii, sem.at[0]), pltpu.make_async_copy(io, gio, sem.at[1])]
    for c in direct:
        c.start()
    f = fac[0:1, 0:1]
    bo[...] = qo[...].astype(F32) * f
    a = pltpu.make_async_copy(bo, gqo, sem.at[2])
    a.start()
    bi[...] = qi[...].astype(F32) * f
    b = pltpu.make_async_copy(bi, gqi, sem.at[3])
    b.start()
    for c in direct + [a, b]:
        c.wait()


def solution(mesh):
    D = mesh.shape["dp"]
    k = D.bit_length() - 1

    def on_device(qf, qw, pos, feat, ids, logq, wqi, wqo, wii, wio):
        Q, FE = qf.shape
        H, E = wqo.shape
        NI = feat.shape[0]
        I = NI * D * 2
        QT, CW, PR = 256, E, FE
        AT = QT if I <= 4 * QT else QT // 2
        parts = I // PR + H // PR + H // CW
        vm = pl.BlockSpec(memory_space=pltpu.VMEM)
        dma = pltpu.SemaphoreType.DMA
        args = (qf, qw, pos.reshape(1, Q), feat, ids.reshape(1, NI), logq.reshape(1, NI), wqi, wqo, wii, wio)
        oqi, oqo, oii, oio, fac = pl.pallas_call(
            functools.partial(kernel, D, k, QT, AT, CW, PR),
            name="retrieval_grads",
            out_shape=(
                jax.ShapeDtypeStruct((FE, H), BF16),
                jax.ShapeDtypeStruct((H, E), BF16),
                jax.ShapeDtypeStruct((FE, H), F32),
                jax.ShapeDtypeStruct((H, E), F32),
                jax.ShapeDtypeStruct((8, 128), F32),
            ),
            in_specs=[pl.BlockSpec(memory_space=pltpu.HBM)] * 10,
            out_specs=(vm,) * 5,
            scratch_shapes=[
                pltpu.VMEM((Q, FE), BF16), pltpu.VMEM((Q,), BF16), pltpu.VMEM((1, Q), jnp.int32),
                pltpu.VMEM((1, NI), jnp.int32), pltpu.VMEM((1, NI), BF16),
                pltpu.VMEM((FE, H), BF16), pltpu.VMEM((H, E), BF16), pltpu.VMEM((FE, H), BF16), pltpu.VMEM((H, E), BF16),
                dma((10,)),
                pltpu.VMEM((D, 2, NI, FE), BF16),
                pltpu.VMEM((D, 2, 8, 128), F32),
                pltpu.VMEM((D, 2, NI, E), BF16),
                pltpu.VMEM((Q, H), F32),
                pltpu.VMEM((Q, H), BF16),
                pltpu.VMEM((H, Q), BF16),
                pltpu.VMEM((FE, Q), BF16),
                pltpu.VMEM((Q, E), BF16),
                pltpu.VMEM((Q, E), BF16),
                pltpu.VMEM((1, Q), F32),
                pltpu.VMEM((I, E), F32),
                pltpu.VMEM((parts, PR, E), BF16),
                pltpu.VMEM((parts, PR + 64, E), BF16),
                pltpu.VMEM((parts, PR, E), BF16),
                dma((D,)), dma((D,)), dma((D,)), dma((D,)), dma((D,)), dma((D,)), dma((3,)), dma((3,)),
                dma((parts, 2 * k + 2)), dma((parts, 2 * k + 2)), dma((parts, 2 * k + 2)), dma((parts, 2 * k + 2)),
            ],
            compiler_params=pltpu.CompilerParams(
                collective_id=0, has_side_effects=True, vmem_limit_bytes=(48 if I <= 4 * QT else 62) * 1024 * 1024),
        )(*[pltpu.with_memory_space_constraint(v, pltpu.HBM) for v in args])
        hbm = pl.BlockSpec(memory_space=pltpu.HBM)
        return tuple(pl.pallas_call(
            finish,
            name="finish",
            out_shape=(
                jax.ShapeDtypeStruct((FE, H), F32),
                jax.ShapeDtypeStruct((H, E), F32),
                jax.ShapeDtypeStruct((FE, H), F32),
                jax.ShapeDtypeStruct((H, E), F32),
            ),
            in_specs=[vm] * 5,
            out_specs=(hbm,) * 4,
            scratch_shapes=[pltpu.VMEM((FE, H), F32), pltpu.VMEM((H, E), F32), pltpu.SemaphoreType.DMA((4,))],
            compiler_params=pltpu.CompilerParams(vmem_limit_bytes=8 * 1024 * 1024),
        )(oqi, oqo, oii, oio, fac))

    rows = P(("dp", "grp"), None)
    flat = P(("dp", "grp"))
    return jax.shard_map(
        on_device, mesh=mesh,
        in_specs=(rows, flat, flat, rows, flat, flat, P(), P(), P(), P()),
        out_specs=(P(), P(), P(), P()),
        check_vma=False,
    )
```

```python
import functools

import jax
import jax.numpy as jnp
from jax import lax
from jax.experimental import pallas as pl
from jax.experimental.pallas import tpu as pltpu
from jax.sharding import PartitionSpec as P

MESH = pl.DeviceIdType.MESH
F32 = jnp.float32
BF16 = jnp.bfloat16
SCALE = 0.25
LOSS = 1024.0
NN = (((1,), (0,)), ((), ()))
NT = (((1,), (1,)), ((), ()))
TN = (((0,), (0,)), ((), ()))


def dot(a, b, dims=NN):
    return lax.dot_general(a, b, dims, preferred_element_type=F32)


def gate_of(v):
    return 1.0 / (1.0 + jnp.exp(-v))


def kernel(
    D, k, QT, AT, CW, PR,
    qf_h, qw_h, pos_h, feat_h, ids_h, logq_h, wqi_h, wqo_h, wii_h, wio_h,
    oqi, oqo, oii, oio, ofac,
    qf, qw, pos, ids, logq, wqi, wqo, wii, wio, load,
    feats, meta, embs, slope, hid, hidT, qfT, qemb, qgrad, wrow, igrad, buf, rcv, gat,
    em_send, em_recv, ag_send, ag_recv, mt_send, mt_recv, pair_send, pair_recv,
    rs_send, rs_recv, fg_send, fg_recv,
):
    dp = lax.axis_index("dp")
    grp = lax.axis_index("grp")
    Q, FE = qf.shape
    H, E = wqo.shape
    NI = feat_h.shape[0]
    I = D * 2 * NI
    other = 1 - grp
    n_item = I // PR
    n_out = H // PR
    n_in = H // CW
    parts = n_item + n_out + n_in

    mine_at = feats.at[dp, grp]
    pairs = [(feat_h, mine_at), (wii_h, wii), (wio_h, wio), (ids_h, ids), (logq_h, logq), (qw_h, qw), (wqi_h, wqi),
             (qf_h, qf), (wqo_h, wqo), (pos_h, pos)]
    loads = [pltpu.make_async_copy(a, b, load.at[i]) for i, (a, b) in enumerate(pairs)]
    for c in loads:
        c.start()

    barrier = pltpu.get_barrier_semaphore()

    def greet(o, c):
        pl.semaphore_signal(barrier, inc=1, device_id=(lax.rem(dp + o, D), grp), device_id_type=MESH)
        return c

    lax.fori_loop(1, D, greet, 0)
    pl.semaphore_signal(barrier, inc=1, device_id=(dp, other), device_id_type=MESH)

    for c in loads[:6]:
        c.wait()
    wrow[...] = qw[...].astype(F32).reshape(1, Q)
    i_pre = dot(mine_at[...], wii[...])
    embs[dp, grp] = dot((i_pre * gate_of(i_pre)).astype(BF16), wio[...]).astype(BF16)
    meta[dp, grp] = jnp.zeros((8, 128), F32)
    meta[dp, grp, 0:1, 0:NI] = ids[...].astype(F32)
    meta[dp, grp, 1:2, 0:NI] = logq[...].astype(F32)
    meta[dp, grp, 2:3, :] = jnp.broadcast_to(jnp.sum(wrow[...], axis=1, keepdims=True), (1, 128))

    pl.semaphore_wait(barrier, D)

    def to_all(ref, send, recv):
        def copy(o):
            return pltpu.make_async_remote_copy(
                src_ref=ref.at[dp, grp], dst_ref=ref.at[dp, grp], send_sem=send.at[o], recv_sem=recv.at[o],
                device_id=(lax.rem(dp + o, D), grp), device_id_type=MESH)

        def start(o, c):
            copy(o).start()
            return c

        def wait(o, c):
            copy(o).wait()
            return c

        return (lambda: lax.fori_loop(1, D, start, 0)), (lambda: lax.fori_loop(1, D, wait, 0))

    def to_pair(ref, i):
        return pltpu.make_async_remote_copy(
            src_ref=ref.at[:, grp], dst_ref=ref.at[:, grp], send_sem=pair_send.at[i], recv_sem=pair_recv.at[i],
            device_id=(dp, other), device_id_type=MESH)

    emb_start, emb_wait = to_all(embs, em_send, em_recv)
    meta_start, meta_wait = to_all(meta, mt_send, mt_recv)
    feat_start, feat_wait = to_all(feats, ag_send, ag_recv)
    meta_start()
    emb_start()
    feat_start()

    for c in loads[6:9]:
        c.wait()

    def forward(t, c):
        rows = pl.ds(pl.multiple_of(t * QT, QT), QT)
        pre = dot(qf[rows, :], wqi[...])
        g = gate_of(pre)
        h = (pre * g).astype(BF16)
        slope[rows, :] = g * (1.0 + pre * (1.0 - g))
        hid[rows, :] = h
        qemb[rows, :] = dot(h, wqo[...]).astype(BF16)
        return c

    lax.fori_loop(0, Q // QT, forward, 0)
    hidT[...] = hid[...].T
    qfT[...] = qf[...].T

    loads[9].wait()
    meta_wait()
    pm = to_pair(meta, 0)
    pm.start()
    emb_wait()
    pe = to_pair(embs, 1)
    pe.start()
    pm.wait()
    pe.wait()

    diag = lax.broadcasted_iota(jnp.int32, (1, NI, 128), 1) == lax.broadcasted_iota(jnp.int32, (1, NI, 128), 2)

    def column(r):
        row = meta[:, :, r:r + 1, :].reshape(2 * D, 1, 128)
        return jnp.sum(jnp.where(diag, row, 0.0), axis=2, keepdims=True).reshape(I, 1)

    id_all = column(0)
    lq_all = column(1)
    total = jnp.sum(meta[:, :, 2:3, :].reshape(2 * D, 128)[:, 0:1], axis=0, keepdims=True)
    factor = LOSS / total
    ofac[...] = jnp.broadcast_to(factor, ofac.shape)

    def attend(t, c):
        rows = pl.ds(pl.multiple_of(t * AT, AT), AT)
        e_t = qemb[rows, :]
        i_emb = embs[...].reshape(I, E)
        s = SCALE * dot(i_emb, e_t, NT) - lq_all
        hit = lax.broadcasted_iota(jnp.int32, (I, AT), 0) == pos[:, rows]
        pid = jnp.sum(jnp.where(hit, id_all, 0.0), axis=0, keepdims=True)
        s = jnp.where(jnp.logical_and(id_all == pid, jnp.logical_not(hit)), -jnp.inf, s)
        m = jnp.maximum(jnp.max(s, axis=0, keepdims=True), -1e30)
        ex = jnp.exp(s - m)
        inv = 1.0 / jnp.sum(ex, axis=0, keepdims=True)
        w = wrow[:, rows]
        d = (w * (ex * inv - jnp.where(hit, 1.0, 0.0))).astype(BF16)
        term = dot(d, e_t)
        igrad[...] = jnp.where(t == 0, term, igrad[...] + term)
        qgrad[rows, :] = (SCALE * dot(d, i_emb, TN)).astype(BF16)
        return c

    igrad[...] = jnp.zeros_like(igrad)
    lax.fori_loop(0, Q // AT, attend, 0)

    bits = list(range(k))
    tail = [[2, 3]] + [[b] for b in bits[4:]] if k >= 4 else [[b] for b in bits[2:]]
    heads = [[[b] for b in bits[:2]], [[b] for b in bits[:2][::-1]]]

    def plan(p):
        steps, off, rows, slot, sem = [], 0, PR, 0, 0
        for group in [None] + heads[p % 2] + tail:
            ways = 2 if group is None else 1 << len(group)
            one = 1 if group is None else 1 << group[0]
            digit = grp if group is None else lax.rem(lax.div(dp, one), ways)
            split = rows // ways >= 16
            size = rows // ways if split else rows
            moves = []
            for o in range(1, ways):
                there = lax.rem(digit + o, ways)
                to = (dp, there) if group is None else (dp + one * (there - digit), grp)
                moves.append((to, off + there * size if split else off, slot, sem))
                slot += size
                sem += 1
            off = off + digit * size if split else off
            rows = size
            steps.append((split, size, off, moves))
        return steps

    plans = [plan(p) for p in range(parts)]
    stages = len(plans[0])
    back = [s for s in range(stages) if plans[0][s][0]][::-1]
    turns = 1 + stages + len(back)

    def at(off, rows):
        return pl.ds(pl.multiple_of(off, 16), rows)

    def out_copies(p, s):
        split, size, keep, moves = plans[p][s]
        return [pltpu.make_async_remote_copy(
            src_ref=buf.at[p, at(send, size)], dst_ref=rcv.at[p, pl.ds(slot, size)],
            send_sem=rs_send.at[p, i], recv_sem=rs_recv.at[p, i], device_id=to, device_id_type=MESH)
            for to, send, slot, i in moves]

    def back_copies(p, s):
        split, size, keep, moves = plans[p][s]
        return [pltpu.make_async_remote_copy(
            src_ref=gat.at[p, at(keep, size)], dst_ref=gat.at[p, at(keep, size)],
            send_sem=fg_send.at[p, i], recv_sem=fg_recv.at[p, i], device_id=to, device_id_type=MESH)
            for to, send, slot, i in moves]

    def start(copies):
        for c in copies:
            c.start()

    def wait(copies):
        for c in copies:
            c.wait()

    def advance(p, n):
        if n == 0:
            start(out_copies(p, 0))
        elif n <= stages:
            s = n - 1
            wait(out_copies(p, s))
            split, size, keep, moves = plans[p][s]
            got = buf[p, at(keep, size)].astype(F32)
            for to, send, slot, i in moves:
                got = got + rcv[p, pl.ds(slot, size)].astype(F32)
            if n < stages:
                buf[p, at(keep, size)] = got.astype(BF16)
                start(out_copies(p, n))
            else:
                gat[p, at(keep, size)] = got.astype(BF16)
                start(back_copies(p, back[0]))
        else:
            i = n - stages - 1
            wait(back_copies(p, back[i]))
            if i + 1 < len(back):
                start(back_copies(p, back[i + 1]))
            elif p in outs:
                oqo[(p - outs[0]) * PR:(p - outs[0] + 1) * PR, :] = gat[p]
            elif p in ins:
                oqi[:, (p - ins[0]) * CW:(p - ins[0] + 1) * CW] = gat[p]

    items = range(n_item)
    outs = range(n_item, n_item + n_out)
    ins = range(n_item + n_out, parts)

    for p in items:
        buf[p] = (SCALE * igrad[p * PR:(p + 1) * PR, :]).astype(BF16)
        advance(p, 0)

    g_out = dot(hidT[...], qgrad[...])
    for j, p in enumerate(outs):
        buf[p] = g_out[j * PR:(j + 1) * PR, :].astype(BF16)
        advance(p, 0)
    for p in items:
        advance(p, 1)

    for j, p in enumerate(ins):
        cols = slice(j * CW, (j + 1) * CW)
        hg = dot(qgrad[...], wqo[cols, :], NT)
        pg = (hg * slope[:, cols]).astype(BF16)
        buf[p] = dot(qfT[...], pg).astype(BF16)
        advance(p, 0)
        if j == 1:
            for q in items:
                advance(q, 2)

    feat_wait()
    pf = to_pair(feats, 2)
    pf.start()
    step_i = 3

    def item_back(j):
        cols = slice(j * CW, (j + 1) * CW)
        x = feats[...].reshape(I, FE)
        ig = gat[0:n_item].reshape(I, E)
        pre = dot(x, wii[:, cols])
        g = gate_of(pre)
        h = (pre * g).astype(BF16)
        oio[cols, :] = dot(h, ig, TN) * factor
        hg = dot(ig, wio[cols, :], NT)
        pg = (hg * (g * (1.0 + pre * (1.0 - g)))).astype(BF16)
        oii[:, cols] = dot(x, pg, TN) * factor

    done = 0
    for n in range(1, turns):
        for p in list(outs) + list(ins):
            advance(p, n)
        if step_i < turns:
            for q in items:
                advance(q, step_i)
            step_i += 1
            if step_i == turns:
                pf.wait()
        elif done < n_in:
            for _ in range(2):
                item_back(done)
                done += 1
    while done < n_in:
        item_back(done)
        done += 1


def finish(qi, qo, ii, io, fac, gqi, gqo, gii, gio, bi, bo, sem):
    direct = [pltpu.make_async_copy(ii, gii, sem.at[0]), pltpu.make_async_copy(io, gio, sem.at[1])]
    for c in direct:
        c.start()
    f = fac[0:1, 0:1]
    bo[...] = qo[...].astype(F32) * f
    a = pltpu.make_async_copy(bo, gqo, sem.at[2])
    a.start()
    bi[...] = qi[...].astype(F32) * f
    b = pltpu.make_async_copy(bi, gqi, sem.at[3])
    b.start()
    for c in direct + [a, b]:
        c.wait()


def solution(mesh):
    D = mesh.shape["dp"]
    k = D.bit_length() - 1

    def on_device(qf, qw, pos, feat, ids, logq, wqi, wqo, wii, wio):
        Q, FE = qf.shape
        H, E = wqo.shape
        NI = feat.shape[0]
        I = NI * D * 2
        QT, CW, PR = 256, E, FE
        AT = QT if I <= 4 * QT else QT // 2
        parts = I // PR + H // PR + H // CW
        vm = pl.BlockSpec(memory_space=pltpu.VMEM)
        dma = pltpu.SemaphoreType.DMA
        args = (qf, qw, pos.reshape(1, Q), feat, ids.reshape(1, NI), logq.reshape(1, NI), wqi, wqo, wii, wio)
        oqi, oqo, oii, oio, fac = pl.pallas_call(
            functools.partial(kernel, D, k, QT, AT, CW, PR),
            name="retrieval_grads",
            out_shape=(
                jax.ShapeDtypeStruct((FE, H), BF16),
                jax.ShapeDtypeStruct((H, E), BF16),
                jax.ShapeDtypeStruct((FE, H), F32),
                jax.ShapeDtypeStruct((H, E), F32),
                jax.ShapeDtypeStruct((8, 128), F32),
            ),
            in_specs=[pl.BlockSpec(memory_space=pltpu.HBM)] * 10,
            out_specs=(vm,) * 5,
            scratch_shapes=[
                pltpu.VMEM((Q, FE), BF16), pltpu.VMEM((Q,), BF16), pltpu.VMEM((1, Q), jnp.int32),
                pltpu.VMEM((1, NI), jnp.int32), pltpu.VMEM((1, NI), BF16),
                pltpu.VMEM((FE, H), BF16), pltpu.VMEM((H, E), BF16), pltpu.VMEM((FE, H), BF16), pltpu.VMEM((H, E), BF16),
                dma((10,)),
                pltpu.VMEM((D, 2, NI, FE), BF16),
                pltpu.VMEM((D, 2, 8, 128), F32),
                pltpu.VMEM((D, 2, NI, E), BF16),
                pltpu.VMEM((Q, H), F32),
                pltpu.VMEM((Q, H), BF16),
                pltpu.VMEM((H, Q), BF16),
                pltpu.VMEM((FE, Q), BF16),
                pltpu.VMEM((Q, E), BF16),
                pltpu.VMEM((Q, E), BF16),
                pltpu.VMEM((1, Q), F32),
                pltpu.VMEM((I, E), F32),
                pltpu.VMEM((parts, PR, E), BF16),
                pltpu.VMEM((parts, PR + 64, E), BF16),
                pltpu.VMEM((parts, PR, E), BF16),
                dma((D,)), dma((D,)), dma((D,)), dma((D,)), dma((D,)), dma((D,)), dma((3,)), dma((3,)),
                dma((parts, 2 * k + 2)), dma((parts, 2 * k + 2)), dma((parts, 2 * k + 2)), dma((parts, 2 * k + 2)),
            ],
            compiler_params=pltpu.CompilerParams(
                collective_id=0, has_side_effects=True, vmem_limit_bytes=(48 if I <= 4 * QT else 62) * 1024 * 1024),
        )(*[pltpu.with_memory_space_constraint(v, pltpu.HBM) for v in args])
        hbm = pl.BlockSpec(memory_space=pltpu.HBM)
        return tuple(pl.pallas_call(
            finish,
            name="finish",
            out_shape=(
                jax.ShapeDtypeStruct((FE, H), F32),
                jax.ShapeDtypeStruct((H, E), F32),
                jax.ShapeDtypeStruct((FE, H), F32),
                jax.ShapeDtypeStruct((H, E), F32),
            ),
            in_specs=[vm] * 5,
            out_specs=(hbm,) * 4,
            scratch_shapes=[pltpu.VMEM((FE, H), F32), pltpu.VMEM((H, E), F32), pltpu.SemaphoreType.DMA((4,))],
            compiler_params=pltpu.CompilerParams(vmem_limit_bytes=8 * 1024 * 1024),
        )(oqi, oqo, oii, oio, fac))

    rows = P(("dp", "grp"), None)
    flat = P(("dp", "grp"))
    return jax.shard_map(
        on_device, mesh=mesh,
        in_specs=(rows, flat, flat, rows, flat, flat, P(), P(), P(), P()),
        out_specs=(P(), P(), P(), P()),
        check_vma=False,
    )
```
